768 devices in a mesh: row: 192 (over y_hi, x, z), col: 4 (over y_lo, core).
Axes of the slice: x: 4, y: 8 (y_hi: 4, y_lo: 2; y = y_hi * 2 + y_lo), z: 12, core: 2. Of those that a mesh axis runs over, the one named last changes fastest.
Arguments:
- features: bfloat16 [49152, 256], P('row', 'col'), may hold values from -6 to 6
- weight: bfloat16 [256, 256], P(None, 'col'), may hold values from -1.5 to 1.5
- bias: float32 [256], P('col'), may hold values from -3 to 3
- adjacency: bfloat16 [384, 32, 128, 128], P('row'), may hold values from 0 to 1.5, as said below
- block_cols: int32 [384, 32], P('row'), may hold values from 0 to 383, as said below
- block_count: int32 [384], P('row'), may hold values from 2 to 32
Outputs:
- hidden_out: bfloat16 [49152, 256], P('row', 'col')
The draws below stay inside these ranges and needn't reach their ends.
Inputs may be any that keep to these rules, and one draw needn't show every extreme that they name: `adjacency`: about two nonzero entries a row in each stored block on average; nonzero entries lie between 0.5 and 1.5. `block_cols`: slot 0 of block row r names block r; slot 1 names its paired block (r + 192) mod 384; every other entry lies within 2 blocks of r; entries may repeat.
All inputs are finite; a program needn't handle non-finite values.
Results may differ from the reference program's by a relative error of at most 0.0085.
Values may be sent and summed in bfloat16 or wider, within the bound.
No kernel may reach another device: no remote copies, remote signals or barrier semaphores. Data moves between devices by JAX's collectives and lax.ppermute only.
A program may use at most 32 MiB of HBM per device.

```python
import jax
import jax.numpy as jnp
from jax import lax

F = 256
G = 256
BLOCK = 128
KMAX = 32
BR_DEV = 2
NBLK = 384
NODES = 49152


def draw_adjacency(key, part):
    key_mask = jax.random.fold_in(key, 31)
    key_value = jax.random.fold_in(key, 32)
    picks = jax.random.randint(key_mask, (NBLK, KMAX, BLOCK, BLOCK), 0, BLOCK)
    values = jax.random.uniform(key_value, (NBLK, KMAX, BLOCK, BLOCK), jnp.float32, 0.5, 1.5)
    return jnp.where(picks < 2, values, 0.0).astype(jnp.bfloat16)


def draw_block_cols(key, part):
    key_near = jax.random.fold_in(key, 11)
    near = jax.random.randint(key_near, (NBLK, KMAX), -BR_DEV, BR_DEV + 1)
    own = jnp.arange(NBLK, dtype=jnp.int32)[:, None]
    slot = jnp.arange(KMAX, dtype=jnp.int32)[None, :]
    nearby = jnp.clip(own + near, 0, NBLK - 1)
    paired = (own + NBLK // 2) % NBLK
    cols = jnp.where(slot == 0, own, jnp.where(slot == 1, paired, nearby))
    return cols.astype(jnp.int32)


def draw_block_count(key, part):
    key_heavy = jax.random.fold_in(key, 21)
    key_light = jax.random.fold_in(key, 22)
    key_where = jax.random.fold_in(key, 23)
    heavy = jax.random.randint(key_heavy, (NBLK,), 0, 4)
    light = jax.random.randint(key_light, (NBLK,), 2, KMAX // 4 + 1)
    counts = jnp.where(heavy == 0, KMAX, light)
    where_full = jax.random.randint(key_where, (), 0, NBLK)
    counts = jnp.where(jnp.arange(NBLK, dtype=jnp.int32) == where_full, KMAX, counts)
    return counts.astype(jnp.int32)


def shard_levels(rng, shape, shards, low, high):
    level = 1.0
    for position, blocks in shards:
        steps = jax.random.uniform(jax.random.fold_in(jax.random.fold_in(rng, 6), position), (blocks,), jnp.float32, low / len(shards), high / len(shards))
        level = level * jnp.repeat(jnp.exp(steps), shape[position] // blocks).reshape((-1,) + (1,) * (len(shape) - 1 - position))
    return level


def noise(key, dims, width, limit, cuts=(), kind=jnp.bfloat16):
    drawn = width * jax.random.normal(key, dims, jnp.float32)
    if cuts:
        drawn = drawn * shard_levels(key, dims, cuts, -0.22, 0.18)
    return jnp.clip(drawn, -limit, limit).astype(kind)


def setup_inputs(seed: int = 0) -> dict:
    splits = jax.random.split(jax.random.key(seed), 7)
    return {
        "features": noise(splits[0], (NODES, F), 1.0, 6.0, ((0, 192), (1, 4))),
        "weight": noise(splits[1], (F, G), 0.25, 1.5, ((1, 4),)),
        "bias": noise(splits[2], (G,), 0.5, 3.0, ((0, 4),), jnp.float32),
        "adjacency": draw_adjacency(jax.random.fold_in(splits[6], 71), 0),
        "block_cols": draw_block_cols(jax.random.fold_in(splits[6], 71), 0),
        "block_count": draw_block_count(jax.random.fold_in(splits[6], 71), 0),
    }


def reference(features, weight, bias, adjacency, block_cols, block_count):
    nblk = adjacency.shape[0]
    kmax = adjacency.shape[1]
    bsize = adjacency.shape[2]
    live = (jnp.arange(kmax, dtype=jnp.int32)[None, :] < block_count[:, None]).astype(jnp.float32)

    def row_degree(item):
        tiles, alive = item
        return 1.0 + jnp.einsum('kij,k->i', tiles.astype(jnp.float32), alive)
    degree = lax.map(row_degree, (adjacency, live)).reshape(-1)
    scale = lax.rsqrt(degree)
    zvals = (jnp.dot(features, weight, preferred_element_type=jnp.float32) * scale[:, None]).astype(jnp.bfloat16)
    blocks = zvals.reshape(nblk, bsize, -1)

    def row_sum(item):
        tiles, cols, alive = item
        picked = blocks[cols].astype(jnp.float32)
        return jnp.einsum('kij,kjf,k->if', tiles.astype(jnp.float32), picked, alive)
    agg = lax.map(row_sum, (adjacency, block_cols, live)).reshape(nblk * bsize, -1)
    result = jax.nn.relu(scale[:, None] * (agg + zvals.astype(jnp.float32)) + bias[None, :])
    return result.astype(jnp.bfloat16)
```

```python
import jax
import jax.numpy as jnp
from jax import lax
from jax.experimental import pallas as pl
from jax.experimental.pallas import tpu as pltpu
from jax.sharding import PartitionSpec as P

F32 = jnp.float32
BF16 = jnp.bfloat16
SMEM = pltpu.MemorySpace.SMEM
VMEM = pltpu.MemorySpace.VMEM
NT = (((1,), (1,)), ((), ()))


def split(value):
    high = value.astype(BF16)
    return high, (value - high.astype(F32)).astype(BF16)


def degree_kernel(count_ref, feat_ref, adj_ref, out_ref, tiles, sums, sem):
    kmax, part, lanes = tiles.shape
    bsize = adj_ref.shape[2]
    col = lax.axis_index("col")
    start = col * part
    r = start // bsize
    offset = pl.multiple_of(lax.rem(start, bsize), part)
    copy = pltpu.make_async_copy(adj_ref.at[r, :, pl.ds(offset, part), :], tiles, sem)
    copy.start()
    rows = feat_ref.shape[0]
    out_ref[:rows, :] = feat_ref[...]
    sums[...] = jnp.zeros_like(sums)
    count = count_ref[r]
    copy.wait()
    total = jnp.zeros((part, lanes), F32)
    for k in range(kmax):
        total += jnp.where(k < count, tiles[k].astype(F32), 0.0)
    total_at = pl.multiple_of(start, part)
    sums[pl.ds(total_at, part), :] = total
    ones = jnp.ones((16, lanes), BF16)
    high, low = split(sums[...])
    degree = 1.0 + (
        lax.dot_general(ones, high, NT, preferred_element_type=F32)
        + lax.dot_general(ones, low, NT, preferred_element_type=F32)
    )
    nodes = degree.shape[1]
    node = lax.broadcasted_iota(jnp.int32, degree.shape, 1)
    row = lax.broadcasted_iota(jnp.int32, degree.shape, 0)
    scale = lax.rsqrt(degree)
    scale = jnp.where((node >= start) & (node < start + part), scale, 0.0)
    high = scale.astype(BF16).astype(F32)
    tail = jnp.where(row == 0, high, jnp.where(row == 1, scale - high, 0.0))
    out_ref[rows:, :] = tail.astype(BF16)


def transform_kernel(gathered_ref, weight_ref, z_ref, scale_ref):
    panels = gathered_ref.shape[0]
    rows = weight_ref.shape[0]
    features = weight_ref.shape[1] // panels
    full = jnp.concatenate([gathered_ref[c, :features, :] for c in range(panels)], axis=0)
    scale = jnp.zeros((1, full.shape[1]), F32)
    for c in range(panels):
        scale += gathered_ref[c, features : features + 1, :].astype(F32)
        scale += gathered_ref[c, features + 1 : features + 2, :].astype(F32)
    product = jnp.dot(weight_ref[...], full, preferred_element_type=F32)
    z_ref[...] = (product * scale).astype(BF16)
    scale_ref[...] = jnp.broadcast_to(scale, scale_ref.shape)


def blocks_kernel(nblk, count_ref, cols_ref, tiles, z_ref, bias_ref, near_ref, base_ref, offset_ref, acc):
    own_rows, _, bsize, _ = tiles.shape
    first = lax.axis_index("row") * own_rows - 2
    acc[...] = jnp.zeros_like(acc)
    features = bias_ref.shape[1]
    eye = lax.broadcasted_iota(jnp.int32, (features, features), 0) == lax.broadcasted_iota(
        jnp.int32, (features, features), 1
    )
    offset_ref[...] = jnp.sum(jnp.where(eye, bias_ref[...], 0.0), axis=1, keepdims=True)
    for r in range(own_rows):
        rows = slice(r * bsize, (r + 1) * bsize)
        acc[6 + r, rows, :] = tiles[r, 1].astype(F32)

        def step(k, _):
            place = lax.rem(cols_ref[r, k] - first + 2 * nblk, nblk)
            place = jnp.clip(place, 0, 5)
            acc[place, rows, :] += tiles[r, k].astype(F32)
            return 0

        step(0, 0)
        lax.fori_loop(2, count_ref[r], step, 0)
    for slot, pair in enumerate((0, 4, 6)):
        for h in range(2):
            near_ref[slot, :, h * bsize : (h + 1) * bsize] = acc[pair + h].astype(BF16)
    own = jnp.concatenate([acc[2].astype(BF16), acc[3].astype(BF16)], axis=1)
    z = z_ref[...]
    base_ref[...] = z.astype(F32) + lax.dot_general(z, own, NT, preferred_element_type=F32)


def finish_kernel(before_ref, after_ref, pair_ref, near_ref, base_ref, scale_ref, offset_ref, out_ref):
    total = base_ref[...]
    for slot, ref in enumerate((before_ref, after_ref, pair_ref)):
        total += lax.dot_general(ref[...], near_ref[slot], NT, preferred_element_type=F32)
    result = scale_ref[:1, :] * total + offset_ref[...]
    out_ref[...] = jnp.maximum(result, 0.0).astype(BF16)


def on_device(features, weight, bias, adjacency, block_cols, block_count):
    own_rows, kmax, bsize, _ = adjacency.shape
    devices = lax.axis_size("row")
    panels = lax.axis_size("col")
    nblk = devices * own_rows
    nodes, width = features.shape
    outs = weight.shape[1]
    part = nodes // panels
    vmem = pl.BlockSpec(memory_space=VMEM)
    smem = pl.BlockSpec(memory_space=SMEM)
    hbm = pl.BlockSpec(memory_space=pltpu.MemorySpace.HBM)

    sent = pl.pallas_call(
        degree_kernel,
        out_shape=jax.ShapeDtypeStruct((width + 16, nodes), BF16),
        in_specs=[smem, vmem, hbm],
        out_specs=vmem,
        scratch_shapes=[
            pltpu.VMEM((kmax, part, bsize), BF16),
            pltpu.VMEM((nodes, bsize), F32),
            pltpu.SemaphoreType.DMA,
        ],
        compiler_params=pltpu.CompilerParams(vmem_limit_bytes=4 << 20),
        name="degree",
    )(block_count, features.T, adjacency)
    gathered = lax.all_gather(sent, "col", axis=0, tiled=False)
    z, scale = pl.pallas_call(
        transform_kernel,
        out_shape=(
            jax.ShapeDtypeStruct((outs, nodes), BF16),
            jax.ShapeDtypeStruct((8, nodes), F32),
        ),
        in_specs=[vmem, vmem],
        out_specs=(vmem, vmem),
        compiler_params=pltpu.CompilerParams(vmem_limit_bytes=4 << 20),
        name="transform",
    )(gathered, weight.T)

    def shift(step):
        return lax.ppermute(z, "row", [(s, (s + step) % devices) for s in range(devices)])

    pair, before, after = shift(devices // 2), shift(1), shift(-1)
    near, base, offset = pl.pallas_call(
        lambda *refs: blocks_kernel(nblk, *refs),
        out_shape=(
            jax.ShapeDtypeStruct((3, nodes, 2 * bsize), BF16),
            jax.ShapeDtypeStruct((outs, nodes), F32),
            jax.ShapeDtypeStruct((outs, 1), F32),
        ),
        in_specs=[smem, smem, vmem, vmem, vmem],
        out_specs=(vmem, vmem, vmem),
        scratch_shapes=[pltpu.VMEM((8, nodes, bsize), F32)],
        cost_estimate=pl.CostEstimate(flops=70_000_000, bytes_accessed=2_500_000, transcendentals=0),
        compiler_params=pltpu.CompilerParams(vmem_limit_bytes=12 << 20),
        name="blocks",
    )(block_count, block_cols, adjacency, z, bias.reshape(1, -1))
    out = pl.pallas_call(
        finish_kernel,
        out_shape=jax.ShapeDtypeStruct((outs, nodes), BF16),
        in_specs=[vmem] * 7,
        out_specs=vmem,
        compiler_params=pltpu.CompilerParams(vmem_limit_bytes=4 << 20),
        name="finish",
    )(before, after, pair, near, base, scale, offset)
    return out.T


def solution(mesh):
    return jax.shard_map(
        on_device,
        mesh=mesh,
        in_specs=(
            P("row", "col"),
            P(None, "col"),
            P("col"),
            P("row", None, None, None),
            P("row", None),
            P("row"),
        ),
        out_specs=P("row", "col"),
        check_vma=False,
    )
```

```python
import jax
import jax.numpy as jnp
from jax import lax
from jax.experimental import pallas as pl
from jax.experimental.pallas import tpu as pltpu
from jax.sharding import PartitionSpec as P

F32 = jnp.float32
BF16 = jnp.bfloat16
SMEM = pltpu.MemorySpace.SMEM
VMEM = pltpu.MemorySpace.VMEM
NT = (((1,), (1,)), ((), ()))
LINE = 12


def split(value):
    high = value.astype(BF16)
    return high, (value - high.astype(F32)).astype(BF16)


def degree_kernel(count_hbm, feat_hbm, adj_hbm, out_ref, counts, tiles, sums, sems):
    kmax, part, lanes = tiles.shape
    bsize = adj_hbm.shape[2]
    rows = feat_hbm.shape[0]
    start = lax.axis_index("col") * part
    r = start // bsize
    offset = pl.multiple_of(lax.rem(start, bsize), part)
    half = kmax // 2
    loads = [pltpu.make_async_copy(count_hbm, counts, sems.at[0])]
    for h in range(2):
        ks = pl.ds(h * half, half)
        loads.append(
            pltpu.make_async_copy(adj_hbm.at[r, ks, pl.ds(offset, part), :], tiles.at[ks], sems.at[1 + h])
        )
    loads.append(pltpu.make_async_copy(feat_hbm, out_ref.at[pl.ds(0, rows), :], sems.at[3]))
    for load in loads:
        load.start()
    sums[...] = jnp.zeros_like(sums)
    loads[0].wait()
    count = counts[r]
    total = jnp.zeros((part, lanes), F32)
    for h in range(2):
        loads[1 + h].wait()
        for k in range(h * half, (h + 1) * half):
            total += jnp.where(k < count, tiles[k].astype(F32), 0.0)
    sums[pl.ds(pl.multiple_of(start, part), part), :] = total
    ones = jnp.ones((16, lanes), BF16)
    high, low = split(sums[...])
    degree = 1.0 + (
        lax.dot_general(ones, high, NT, preferred_element_type=F32)
        + lax.dot_general(ones, low, NT, preferred_element_type=F32)
    )
    node = lax.broadcasted_iota(jnp.int32, degree.shape, 1)
    row = lax.broadcasted_iota(jnp.int32, degree.shape, 0)
    scale = lax.rsqrt(degree)
    scale = jnp.where((node >= start) & (node < start + part), scale, 0.0)
    high = scale.astype(BF16).astype(F32)
    tail = jnp.where(row == 0, high, jnp.where(row == 1, scale - high, 0.0))
    out_ref[rows:, :] = tail.astype(BF16)
    loads[3].wait()


def transform_kernel(gathered_ref, weight_ref, z_ref, scale_ref):
    panels = gathered_ref.shape[0]
    rows = weight_ref.shape[0]
    features = weight_ref.shape[1] // panels
    full = jnp.concatenate([gathered_ref[c, :features, :] for c in range(panels)], axis=0)
    scale = jnp.zeros((1, full.shape[1]), F32)
    for c in range(panels):
        scale += gathered_ref[c, features : features + 1, :].astype(F32)
        scale += gathered_ref[c, features + 1 : features + 2, :].astype(F32)
    product = jnp.dot(weight_ref[...], full, preferred_element_type=F32)
    z_ref[...] = (product * scale).astype(BF16)
    scale_ref[...] = jnp.broadcast_to(scale, scale_ref.shape)


def blocks_kernel(count_ref, cols_ref, tiles, z_ref, bias_ref, near_ref, base_ref, offset_ref, same_ref, acc):
    own_rows, _, bsize, _ = tiles.shape
    first = lax.axis_index("row") * own_rows - 2
    acc[...] = jnp.zeros_like(acc)
    features = bias_ref.shape[1]
    eye = lax.broadcasted_iota(jnp.int32, (features, features), 0) == lax.broadcasted_iota(
        jnp.int32, (features, features), 1
    )
    offset_ref[...] = jnp.sum(jnp.where(eye, bias_ref[...], 0.0), axis=1, keepdims=True)
    for r in range(own_rows):
        rows = slice(r * bsize, (r + 1) * bsize)
        acc[6 + r, rows, :] = tiles[r, 1].astype(F32)

        def step(k, _):
            place = jnp.clip(cols_ref[r, k] - first, 0, 5)
            acc[place, rows, :] += tiles[r, k].astype(F32)
            return 0

        step(0, 0)
        lax.fori_loop(2, count_ref[r], step, 0)
    for slot, pair in enumerate((0, 4, 6)):
        for h in range(2):
            near_ref[slot, :, h * bsize : (h + 1) * bsize] = acc[pair + h].astype(BF16)
    own = jnp.concatenate([acc[2].astype(BF16), acc[3].astype(BF16)], axis=1)
    z = z_ref[...]
    same_ref[...] = z
    base_ref[...] = z.astype(F32) + lax.dot_general(z, own, NT, preferred_element_type=F32)


def finish_kernel(
    after_ref, before_ref, first_ref, last_ref, near_ref, base_ref, scale_ref, offset_ref, out_ref
):
    total = base_ref[...]
    for slot, z in enumerate((before_ref[...], after_ref[...], first_ref[...] + last_ref[...])):
        total += lax.dot_general(z, near_ref[slot], NT, preferred_element_type=F32)
    result = scale_ref[:1, :] * total + offset_ref[...]
    out_ref[...] = jnp.maximum(result, 0.0).astype(BF16)


def on_device(features, weight, bias, adjacency, block_cols, block_count):
    own_rows, kmax, bsize, _ = adjacency.shape
    devices = lax.axis_size("row")
    panels = lax.axis_size("col")
    nodes, width = features.shape
    outs = weight.shape[1]
    part = nodes // panels
    vmem = pl.BlockSpec(memory_space=VMEM)
    smem = pl.BlockSpec(memory_space=SMEM)
    hbm = pl.BlockSpec(memory_space=pltpu.MemorySpace.HBM)

    sent = pl.pallas_call(
        degree_kernel,
        out_shape=jax.ShapeDtypeStruct((width + 16, nodes), BF16),
        in_specs=[hbm, hbm, hbm],
        out_specs=vmem,
        scratch_shapes=[
            pltpu.SMEM((own_rows,), jnp.int32),
            pltpu.VMEM((kmax, part, bsize), BF16),
            pltpu.VMEM((nodes, bsize), F32),
            pltpu.SemaphoreType.DMA((4,)),
        ],
        compiler_params=pltpu.CompilerParams(vmem_limit_bytes=62_000_000),
        name="degree",
    )(block_count, features.T, adjacency)
    gathered = lax.all_gather(sent, "col", axis=0, tiled=False)
    z, scale = pl.pallas_call(
        transform_kernel,
        out_shape=(
            jax.ShapeDtypeStruct((outs, nodes), BF16),
            jax.ShapeDtypeStruct((8, nodes), F32),
        ),
        in_specs=[vmem, vmem],
        out_specs=(vmem, vmem),
        compiler_params=pltpu.CompilerParams(vmem_limit_bytes=4 << 20),
        name="transform",
    )(gathered, weight.T)

    def exchange(values, targets):
        return lax.ppermute(values, "row", [(s, targets(s)) for s in range(devices) if targets(s) is not None])

    half = devices // 2
    line = LINE
    opposite_first = exchange(z, lambda s: (s + half) % devices if s % line < line // 2 else None)
    before = exchange(z, lambda s: s + 1 if s + 1 < devices else None)
    after = exchange(z, lambda s: s - 1 if s > 0 else None)
    near, base, offset, same = pl.pallas_call(
        blocks_kernel,
        out_shape=(
            jax.ShapeDtypeStruct((3, nodes, 2 * bsize), BF16),
            jax.ShapeDtypeStruct((outs, nodes), F32),
            jax.ShapeDtypeStruct((outs, 1), F32),
            jax.ShapeDtypeStruct((outs, nodes), BF16),
        ),
        in_specs=[smem, smem, vmem, vmem, vmem],
        out_specs=(vmem, vmem, vmem, vmem),
        scratch_shapes=[pltpu.VMEM((8, nodes, bsize), F32)],
        cost_estimate=pl.CostEstimate(flops=70_000_000, bytes_accessed=2_500_000, transcendentals=0),
        compiler_params=pltpu.CompilerParams(vmem_limit_bytes=12 << 20),
        name="blocks",
    )(block_count, block_cols, adjacency, z, bias.reshape(1, -1))
    opposite_last = exchange(same, lambda s: None if s % line < line // 2 else (s + half) % devices)
    out = pl.pallas_call(
        finish_kernel,
        out_shape=jax.ShapeDtypeStruct((outs, nodes), BF16),
        in_specs=[vmem] * 8,
        out_specs=vmem,
        compiler_params=pltpu.CompilerParams(vmem_limit_bytes=4 << 20),
        name="finish",
    )(after, before, opposite_first, opposite_last, near, base, scale, offset)
    return out.T


def solution(mesh):
    return jax.shard_map(
        on_device,
        mesh=mesh,
        in_specs=(
            P("row", "col"),
            P(None, "col"),
            P("col"),
            P("row", None, None, None),
            P("row", None),
            P("row"),
        ),
        out_specs=P("row", "col"),
        check_vma=False,
    )
```

```python
import jax
import jax.numpy as jnp
from jax import lax
from jax.experimental import pallas as pl
from jax.experimental.pallas import tpu as pltpu
from jax.sharding import PartitionSpec as P

F32 = jnp.float32
BF16 = jnp.bfloat16
SMEM = pltpu.MemorySpace.SMEM
VMEM = pltpu.MemorySpace.VMEM
NT = (((1,), (1,)), ((), ()))
LINE = 12
NEAR = 6


def split(value):
    high = value.astype(BF16)
    return high, (value - high.astype(F32)).astype(BF16)


def clear_kernel(out_ref):
    out_ref[...] = jnp.zeros_like(out_ref)


def transform_kernel(
    count_ref, cols_ref, tiles, full_ref, weight_ref, bias_ref, _, z_ref, blocks_ref, scale_ref, offset_ref
):
    own_rows, _, bsize, _ = tiles.shape
    first = lax.axis_index("row") * own_rows - 2
    for r in range(own_rows):
        rows = slice(r * bsize, (r + 1) * bsize)
        blocks_ref[6 + r, rows, :] = tiles[r, 1]

        def step(k, _):
            place = jnp.clip(cols_ref[r, k] - first, 0, 5)
            blocks_ref[place, rows, :] += tiles[r, k]
            return 0

        step(0, 0)
        lax.fori_loop(2, count_ref[r], step, 0)
    total = blocks_ref[0].astype(F32)
    for b in range(1, blocks_ref.shape[0]):
        total += blocks_ref[b].astype(F32)
    ones = jnp.ones((16, bsize), BF16)
    high, low = split(total)
    degree = 1.0 + (
        lax.dot_general(ones, high, NT, preferred_element_type=F32)
        + lax.dot_general(ones, low, NT, preferred_element_type=F32)
    )
    scale = lax.rsqrt(degree[:1, :])
    product = jnp.dot(weight_ref[...], full_ref[...], preferred_element_type=F32)
    z_ref[...] = (product * scale).astype(BF16)
    scale_ref[...] = jnp.broadcast_to(scale, scale_ref.shape)
    outs = bias_ref.shape[1]
    eye = lax.broadcasted_iota(jnp.int32, (outs, outs), 0) == lax.broadcasted_iota(jnp.int32, (outs, outs), 1)
    offset_ref[...] = jnp.sum(jnp.where(eye, bias_ref[...], 0.0), axis=1, keepdims=True)


def finish_kernel(
    last_ref, after_ref, first_ref, before_ref, z_ref, blocks_ref, scale_ref, offset_ref, out_ref
):
    own = z_ref[...]
    total = own.astype(F32)
    before = before_ref[...]
    after = after_ref[...]
    pair = first_ref[...] + last_ref[...]
    for slot, z in enumerate((before, own, after, pair)):
        block = jnp.concatenate([blocks_ref[2 * slot], blocks_ref[2 * slot + 1]], axis=1)
        total += lax.dot_general(z, block, NT, preferred_element_type=F32)
    result = scale_ref[:1, :] * total + offset_ref[...]
    out_ref[...] = jnp.maximum(result, 0.0).astype(BF16)


def on_device(features, weight, bias, adjacency, block_cols, block_count):
    own_rows, _, bsize, _ = adjacency.shape
    devices = lax.axis_size("row")
    nodes = features.shape[0]
    outs = weight.shape[1]
    vmem = pl.BlockSpec(memory_space=VMEM)
    smem = pl.BlockSpec(memory_space=SMEM)

    cleared = pl.pallas_call(
        clear_kernel,
        out_shape=jax.ShapeDtypeStruct((8, nodes, bsize), BF16),
        out_specs=vmem,
        compiler_params=pltpu.CompilerParams(vmem_limit_bytes=4 << 20),
        cost_estimate=pl.CostEstimate(flops=1 << 32, bytes_accessed=64 << 20, transcendentals=0),
        name="clear",
    )()
    panel, cleared = lax.optimization_barrier((features.T, cleared))
    full = lax.all_gather(panel, "col", axis=0, tiled=True)
    z, blocks, scale, offset = pl.pallas_call(
        transform_kernel,
        out_shape=(
            jax.ShapeDtypeStruct((outs, nodes), BF16),
            jax.ShapeDtypeStruct((8, nodes, bsize), BF16),
            jax.ShapeDtypeStruct((8, nodes), F32),
            jax.ShapeDtypeStruct((outs, 1), F32),
        ),
        in_specs=[smem, smem, vmem, vmem, vmem, vmem, vmem],
        input_output_aliases={6: 1},
        out_specs=(vmem,) * 4,
        compiler_params=pltpu.CompilerParams(vmem_limit_bytes=12 << 20),
        name="transform",
    )(block_count, block_cols, adjacency, full, weight.T, bias.reshape(1, -1), cleared)

    def exchange(targets):
        return lax.ppermute(z, "row", [(s, targets(s)) for s in range(devices) if targets(s) is not None])

    half = devices // 2

    def plus(s):
        return s + 1 if s + 1 < devices else None

    def minus(s):
        return s - 1 if s > 0 else None

    def pair(s):
        return (s + half) % devices

    before = exchange(plus)
    first = exchange(lambda s: pair(s) if s % LINE < NEAR or (s >= half and s % LINE < LINE - 1) else None)
    after = exchange(minus)
    last = exchange(lambda s: pair(s) if s % LINE == LINE - 1 or (s < half and s % LINE >= NEAR) else None)
    out = pl.pallas_call(
        finish_kernel,
        out_shape=jax.ShapeDtypeStruct((outs, nodes), BF16),
        in_specs=[vmem] * 8,
        out_specs=vmem,
        compiler_params=pltpu.CompilerParams(vmem_limit_bytes=4 << 20),
        name="finish",
    )(last, after, first, before, z, blocks, scale, offset)
    return out.T


def solution(mesh):
    return jax.shard_map(
        on_device,
        mesh=mesh,
        in_specs=(
            P("row", "col"),
            P(None, "col"),
            P("col"),
            P("row", None, None, None),
            P("row", None),
            P("row"),
        ),
        out_specs=P("row", "col"),
        check_vma=False,
    )
```

```python
import jax
import jax.numpy as jnp
from jax import lax
from jax.experimental import pallas as pl
from jax.experimental.pallas import tpu as pltpu
from jax.sharding import PartitionSpec as P

F32 = jnp.float32
BF16 = jnp.bfloat16
SMEM = pltpu.MemorySpace.SMEM
VMEM = pltpu.MemorySpace.VMEM
NT = (((1,), (1,)), ((), ()))
LINE = 12
NEAR = 6
UNROLL = 3


def split(value):
    high = value.astype(BF16)
    return high, (value - high.astype(F32)).astype(BF16)


def clear_kernel(*out_refs):
    for ref in out_refs:
        ref[...] = jnp.zeros_like(ref)


def transform_kernel(
    count_ref, cols_ref, tiles, full_ref, weight_ref, bias_ref, _a, _b, z_ref, *refs
):
    *blocks, scale_ref, offset_ref = refs
    own_rows, _, bsize, _ = tiles.shape
    first = lax.axis_index("row") * own_rows - 2
    spare = blocks[0].shape[0] - 1
    counts = [count_ref[r] for r in range(own_rows)]

    def add(r, k):
        place = jnp.where(k < counts[r], jnp.clip(cols_ref[r, k] - first, 0, 5), spare)
        blocks[r][place] += tiles[r, k]

    for r in range(own_rows):
        blocks[r][6 + r] = tiles[r, 1]
        add(r, 0)

    def step(k, _):
        for u in range(UNROLL):
            for r in range(own_rows):
                add(r, 2 + k * UNROLL + u)
        return 0

    longest = jnp.maximum(counts[0], counts[1])
    lax.fori_loop(0, (longest - 2 + UNROLL - 1) // UNROLL, step, 0)
    sums = []
    for r in range(own_rows):
        total = blocks[r][0].astype(F32)
        for b in range(1, spare):
            total += blocks[r][b].astype(F32)
        sums.append(total)
    total = jnp.concatenate(sums, axis=0)
    ones = jnp.ones((16, bsize), BF16)
    high, low = split(total)
    degree = 1.0 + (
        lax.dot_general(ones, high, NT, preferred_element_type=F32)
        + lax.dot_general(ones, low, NT, preferred_element_type=F32)
    )
    scale = lax.rsqrt(degree[:1, :])
    product = jnp.dot(weight_ref[...], full_ref[...], preferred_element_type=F32)
    z_ref[...] = (product * scale).astype(BF16)
    scale_ref[...] = jnp.broadcast_to(scale, scale_ref.shape)
    outs = bias_ref.shape[1]
    eye = lax.broadcasted_iota(jnp.int32, (outs, outs), 0) == lax.broadcasted_iota(jnp.int32, (outs, outs), 1)
    offset_ref[...] = jnp.sum(jnp.where(eye, bias_ref[...], 0.0), axis=1, keepdims=True)


def finish_kernel(
    last_ref, after_ref, first_ref, before_ref, z_ref, upper_ref, lower_ref, scale_ref, offset_ref, out_ref
):
    own = z_ref[...]
    total = own.astype(F32)
    before = before_ref[...]
    after = after_ref[...]
    pair = first_ref[...] + last_ref[...]
    for slot, z in enumerate((before, own, after, pair)):
        rows = [jnp.concatenate([ref[2 * slot], ref[2 * slot + 1]], axis=1) for ref in (upper_ref, lower_ref)]
        block = jnp.concatenate(rows, axis=0)
        total += lax.dot_general(z, block, NT, preferred_element_type=F32)
    result = scale_ref[:1, :] * total + offset_ref[...]
    out_ref[...] = jnp.maximum(result, 0.0).astype(BF16)


def on_device(features, weight, bias, adjacency, block_cols, block_count):
    own_rows, _, bsize, _ = adjacency.shape
    devices = lax.axis_size("row")
    nodes = features.shape[0]
    outs = weight.shape[1]
    vmem = pl.BlockSpec(memory_space=VMEM)
    smem = pl.BlockSpec(memory_space=SMEM)

    sums = jax.ShapeDtypeStruct((9, bsize, bsize), BF16)
    cleared = pl.pallas_call(
        clear_kernel,
        out_shape=(sums,) * own_rows,
        out_specs=(vmem,) * own_rows,
        compiler_params=pltpu.CompilerParams(vmem_limit_bytes=4 << 20),
        cost_estimate=pl.CostEstimate(flops=550_000_000, bytes_accessed=1 << 20, transcendentals=0),
        name="clear",
    )()
    panel, cleared = lax.optimization_barrier((features.T, cleared))
    full = lax.all_gather(panel, "col", axis=0, tiled=True)
    z, upper, lower, scale, offset = pl.pallas_call(
        transform_kernel,
        out_shape=(
            jax.ShapeDtypeStruct((outs, nodes), BF16),
            sums,
            sums,
            jax.ShapeDtypeStruct((8, nodes), F32),
            jax.ShapeDtypeStruct((outs, 1), F32),
        ),
        in_specs=[smem, smem] + [vmem] * 6,
        input_output_aliases={6: 1, 7: 2},
        out_specs=(vmem,) * 5,
        compiler_params=pltpu.CompilerParams(vmem_limit_bytes=12 << 20),
        name="transform",
    )(block_count, block_cols, adjacency, full, weight.T, bias.reshape(1, -1), *cleared)

    def exchange(targets):
        return lax.ppermute(z, "row", [(s, targets(s)) for s in range(devices) if targets(s) is not None])

    half = devices // 2

    def plus(s):
        return s + 1 if s + 1 < devices else None

    def minus(s):
        return s - 1 if s > 0 else None

    def pair(s):
        return (s + half) % devices

    before = exchange(plus)
    first = exchange(lambda s: pair(s) if s % LINE < NEAR or (s >= half and s % LINE < LINE - 1) else None)
    after = exchange(minus)
    last = exchange(lambda s: pair(s) if s % LINE == LINE - 1 or (s < half and s % LINE >= NEAR) else None)
    out = pl.pallas_call(
        finish_kernel,
        out_shape=jax.ShapeDtypeStruct((outs, nodes), BF16),
        in_specs=[vmem] * 9,
        out_specs=vmem,
        compiler_params=pltpu.CompilerParams(vmem_limit_bytes=4 << 20),
        name="finish",
    )(last, after, first, before, z, upper, lower, scale, offset)
    return out.T


def solution(mesh):
    return jax.shard_map(
        on_device,
        mesh=mesh,
        in_specs=(
            P("row", "col"),
            P(None, "col"),
            P("col"),
            P("row", None, None, None),
            P("row", None),
            P("row"),
        ),
        out_specs=P("row", "col"),
        check_vma=False,
    )
```

```python
import functools

import jax
import jax.numpy as jnp
from jax import lax
from jax.experimental import pallas as pl
from jax.experimental.pallas import tpu as pltpu
from jax.sharding import PartitionSpec as P

F32 = jnp.float32
BF16 = jnp.bfloat16
VMEM = pltpu.MemorySpace.VMEM
NT = (((1,), (1,)), ((), ()))
LINE = 12
NEAR = 6
UNROLL = 3


def split(value):
    high = value.astype(BF16)
    return high, (value - high.astype(F32)).astype(BF16)


def clear_kernel(*out_refs):
    for ref in out_refs:
        ref[...] = jnp.zeros_like(ref)


def transform_kernel(count_ref, tiles, full_ref, weight_ref, z_ref, scale_ref):
    own_rows, kmax, bsize, _ = tiles.shape
    product = jnp.dot(weight_ref[...], full_ref[...], preferred_element_type=F32)
    sums = []
    for r in range(own_rows):
        count = jnp.broadcast_to(count_ref[:, r : r + 1], (8, bsize))
        total = jnp.zeros((bsize // 8, 8, bsize), F32)
        for k in range(kmax):
            live = jnp.where(count > k, 1.0, 0.0)
            total += tiles[r, k].astype(F32).reshape(total.shape) * live[None]
        sums.append(total.reshape(bsize, bsize))
    parts = jnp.concatenate(split(jnp.concatenate(sums, axis=0)), axis=1)
    ones = jnp.ones((16, 2 * bsize), BF16)
    degree = 1.0 + lax.dot_general(ones, parts, NT, preferred_element_type=F32)
    scale = lax.rsqrt(degree[:1, :])
    z_ref[...] = (product * scale).astype(BF16)
    scale_ref[...] = jnp.broadcast_to(scale, scale_ref.shape)


def square(blocks, slot):
    rows = [jnp.concatenate([ref[2 * slot], ref[2 * slot + 1]], axis=1) for ref in blocks]
    return jnp.concatenate(rows, axis=0)


def blocks_kernel(mine, count_any, cols_any, tiles, z_ref, bias_ref, *refs):
    upper_ref, lower_ref, base_ref, offset_ref, same_ref, count_ref, cols_ref, sems = refs[-8:]
    same_ref[...] = z_ref[...]

    @pl.when(mine(lax.rem(lax.axis_index("row"), LINE)))
    def _():
        loads = [
            pltpu.make_async_copy(count_any, count_ref, sems.at[0]),
            pltpu.make_async_copy(cols_any, cols_ref, sems.at[1]),
        ]
        for load in loads:
            load.start()
        for load in loads:
            load.wait()
        blocks = (upper_ref, lower_ref)
        own_rows = tiles.shape[0]
        first = lax.axis_index("row") * own_rows - 2
        spare = upper_ref.shape[0] - 1
        counts = [count_ref[r] for r in range(own_rows)]

        def add(r, k):
            place = jnp.where(k < counts[r], jnp.clip(cols_ref[r, k] - first, 0, 5), spare)
            blocks[r][place] += tiles[r, k]

        for r in range(own_rows):
            blocks[r][6 + r] = tiles[r, 1]
            add(r, 0)

        def step(k, _):
            for u in range(UNROLL):
                for r in range(own_rows):
                    add(r, 2 + k * UNROLL + u)
            return 0

        longest = jnp.maximum(counts[0], counts[1])
        lax.fori_loop(0, (longest - 2 + UNROLL - 1) // UNROLL, step, 0)
        own = z_ref[...]
        base_ref[...] = own.astype(F32) + lax.dot_general(own, square(blocks, 1), NT, preferred_element_type=F32)
        outs = bias_ref.shape[1]
        eye = lax.broadcasted_iota(jnp.int32, (outs, outs), 0) == lax.broadcasted_iota(jnp.int32, (outs, outs), 1)
        offset_ref[...] = jnp.sum(jnp.where(eye, bias_ref[...], 0.0), axis=1, keepdims=True)


def finish_kernel(
    last_ref, after_ref, first_ref, before_ref, upper_ref, lower_ref, base_ref, scale_ref, offset_ref, out_ref
):
    blocks = (upper_ref, lower_ref)
    total = base_ref[...]
    pair = first_ref[...] + last_ref[...]
    for slot, z in ((0, before_ref[...]), (2, after_ref[...]), (3, pair)):
        total += lax.dot_general(z, square(blocks, slot), NT, preferred_element_type=F32)
    result = scale_ref[:1, :] * total + offset_ref[...]
    out_ref[...] = jnp.maximum(result, 0.0).astype(BF16)


def on_device(features, weight, bias, adjacency, block_cols, block_count):
    own_rows, _, bsize, _ = adjacency.shape
    devices = lax.axis_size("row")
    nodes = features.shape[0]
    outs = weight.shape[1]
    vmem = pl.BlockSpec(memory_space=VMEM)
    anywhere = pl.BlockSpec(memory_space=pl.ANY)

    sums = jax.ShapeDtypeStruct((9, bsize, bsize), BF16)
    cleared = pl.pallas_call(
        clear_kernel,
        out_shape=(sums,) * own_rows,
        out_specs=(vmem,) * own_rows,
        compiler_params=pltpu.CompilerParams(vmem_limit_bytes=4 << 20),
        cost_estimate=pl.CostEstimate(flops=550_000_000, bytes_accessed=1 << 20, transcendentals=0),
        name="clear",
    )()
    panel, cleared = lax.optimization_barrier((features.T, cleared))
    full = lax.all_gather(panel, "col", axis=0, tiled=True)
    z, scale = pl.pallas_call(
        transform_kernel,
        out_shape=(
            jax.ShapeDtypeStruct((outs, nodes), BF16),
            jax.ShapeDtypeStruct((8, nodes), F32),
        ),
        in_specs=[vmem] * 4,
        out_specs=(vmem,) * 2,
        compiler_params=pltpu.CompilerParams(vmem_limit_bytes=12 << 20),
        name="transform",
    )(block_count.reshape(1, -1), adjacency, full, weight.T)

    half = devices // 2

    def plus(s):
        return s + 1 if s + 1 < devices else None

    def minus(s):
        return s - 1 if s > 0 else None

    def pair(s):
        return (s + half) % devices

    def sum_blocks(mine, values, kept):
        shapes = (
            sums,
            sums,
            jax.ShapeDtypeStruct((outs, nodes), F32),
            jax.ShapeDtypeStruct((outs, 1), F32),
            jax.ShapeDtypeStruct((outs, nodes), BF16),
        )
        return pl.pallas_call(
            functools.partial(blocks_kernel, mine),
            out_shape=shapes,
            in_specs=[anywhere, anywhere] + [vmem] * (3 + len(kept)),
            input_output_aliases={5 + i: i for i in range(len(kept))},
            out_specs=(vmem,) * 5,
            scratch_shapes=[
                pltpu.SMEM(block_count.shape, jnp.int32),
                pltpu.SMEM(block_cols.shape, jnp.int32),
                pltpu.SemaphoreType.DMA((2,)),
            ],
            compiler_params=pltpu.CompilerParams(vmem_limit_bytes=12 << 20),
            cost_estimate=pl.CostEstimate(flops=50_000_000, bytes_accessed=3 << 20, transcendentals=0),
            name="blocks",
        )(block_count, block_cols, adjacency, values, bias.reshape(1, -1), *kept)

    *kept, z = sum_blocks(lambda place: place < NEAR, z, cleared)

    def exchange(targets):
        return lax.ppermute(z, "row", [(s, targets(s)) for s in range(devices) if targets(s) is not None])

    before = exchange(plus)
    first = exchange(lambda s: pair(s) if s % LINE < NEAR or (s >= half and s % LINE < LINE - 1) else None)
    after = exchange(minus)
    last = exchange(lambda s: pair(s) if s % LINE == LINE - 1 or (s < half and s % LINE >= NEAR) else None)
    upper, lower, base, offset, _ = sum_blocks(lambda place: place >= NEAR, z, kept)
    out = pl.pallas_call(
        finish_kernel,
        out_shape=jax.ShapeDtypeStruct((outs, nodes), BF16),
        in_specs=[vmem] * 9,
        out_specs=vmem,
        compiler_params=pltpu.CompilerParams(vmem_limit_bytes=4 << 20),
        name="finish",
    )(last, after, first, before, upper, lower, base, scale, offset)
    return out.T


def solution(mesh):
    return jax.shard_map(
        on_device,
        mesh=mesh,
        in_specs=(
            P("row", "col"),
            P(None, "col"),
            P("col"),
            P("row", None, None, None),
            P("row", None),
            P("row"),
        ),
        out_specs=P("row", "col"),
        check_vma=False,
    )
```

```python
import functools

import jax
import jax.numpy as jnp
from jax import lax
from jax.experimental import pallas as pl
from jax.experimental.pallas import tpu as pltpu
from jax.sharding import PartitionSpec as P

F32 = jnp.float32
BF16 = jnp.bfloat16
VMEM = pltpu.MemorySpace.VMEM
NT = (((1,), (1,)), ((), ()))
LINE = 12
NEAR = 6
UNROLL = 3


def split(value):
    high = value.astype(BF16)
    return high, (value - high.astype(F32)).astype(BF16)


def clear_kernel(*out_refs):
    for ref in out_refs:
        ref[...] = jnp.zeros_like(ref)


def transform_kernel(count_ref, tiles, full_ref, weight_ref, z_ref, scale_ref):
    own_rows, kmax, bsize, _ = tiles.shape
    product = jnp.dot(weight_ref[...], full_ref[...], preferred_element_type=F32)
    sums = []
    for r in range(own_rows):
        count = jnp.broadcast_to(count_ref[:, r : r + 1], (8, bsize))
        total = jnp.zeros((bsize // 8, 8, bsize), F32)
        for k in range(kmax):
            live = jnp.where(count > k, 1.0, 0.0)
            total += tiles[r, k].astype(F32).reshape(total.shape) * live[None]
        sums.append(total.reshape(bsize, bsize))
    parts = jnp.concatenate(split(jnp.concatenate(sums, axis=0)), axis=1)
    ones = jnp.ones((16, 2 * bsize), BF16)
    degree = 1.0 + lax.dot_general(ones, parts, NT, preferred_element_type=F32)
    scale = lax.rsqrt(degree[:1, :])
    z_ref[...] = (product * scale).astype(BF16)
    scale_ref[...] = jnp.broadcast_to(scale, scale_ref.shape)


def square(blocks, slot):
    rows = [jnp.concatenate([ref[2 * slot], ref[2 * slot + 1]], axis=1) for ref in blocks]
    return jnp.concatenate(rows, axis=0)


def blocks_kernel(mine, count_any, cols_any, tiles_any, z_ref, bias_ref, *refs):
    upper_ref, lower_ref, base_ref, offset_ref, same_ref, count_ref, cols_ref, tiles, sems = refs[-9:]
    same_ref[...] = z_ref[...]

    @pl.when(mine(lax.rem(lax.axis_index("row"), LINE)))
    def _():
        loads = [
            pltpu.make_async_copy(count_any, count_ref, sems.at[0]),
            pltpu.make_async_copy(cols_any, cols_ref, sems.at[1]),
            pltpu.make_async_copy(tiles_any, tiles, sems.at[2]),
        ]
        for load in loads:
            load.start()
        for load in loads:
            load.wait()
        blocks = (upper_ref, lower_ref)
        own_rows = tiles.shape[0]
        first = lax.axis_index("row") * own_rows - 2
        spare = upper_ref.shape[0] - 1
        counts = [count_ref[r] for r in range(own_rows)]

        def add(r, k):
            place = jnp.where(k < counts[r], jnp.clip(cols_ref[r, k] - first, 0, 5), spare)
            blocks[r][place] += tiles[r, k]

        for r in range(own_rows):
            blocks[r][6 + r] = tiles[r, 1]
            add(r, 0)

        def step(k, _):
            for u in range(UNROLL):
                for r in range(own_rows):
                    add(r, 2 + k * UNROLL + u)
            return 0

        longest = jnp.maximum(counts[0], counts[1])
        lax.fori_loop(0, (longest - 2 + UNROLL - 1) // UNROLL, step, 0)
        own = z_ref[...]
        base_ref[...] = own.astype(F32) + lax.dot_general(own, square(blocks, 1), NT, preferred_element_type=F32)
        outs = bias_ref.shape[1]
        eye = lax.broadcasted_iota(jnp.int32, (outs, outs), 0) == lax.broadcasted_iota(jnp.int32, (outs, outs), 1)
        offset_ref[...] = jnp.sum(jnp.where(eye, bias_ref[...], 0.0), axis=1, keepdims=True)


def finish_kernel(
    last_ref, after_ref, first_ref, before_ref, upper_ref, lower_ref, base_ref, scale_ref, offset_ref, out_ref
):
    blocks = (upper_ref, lower_ref)
    total = base_ref[...]
    pair = first_ref[...] + last_ref[...]
    for slot, z in ((0, before_ref[...]), (2, after_ref[...]), (3, pair)):
        total += lax.dot_general(z, square(blocks, slot), NT, preferred_element_type=F32)
    result = scale_ref[:1, :] * total + offset_ref[...]
    out_ref[...] = jnp.maximum(result, 0.0).astype(BF16)


def on_device(features, weight, bias, adjacency, block_cols, block_count):
    own_rows, _, bsize, _ = adjacency.shape
    devices = lax.axis_size("row")
    nodes = features.shape[0]
    outs = weight.shape[1]
    vmem = pl.BlockSpec(memory_space=VMEM)
    anywhere = pl.BlockSpec(memory_space=pl.ANY)

    sums = jax.ShapeDtypeStruct((9, bsize, bsize), BF16)
    cleared = pl.pallas_call(
        clear_kernel,
        out_shape=(sums,) * own_rows,
        out_specs=(vmem,) * own_rows,
        compiler_params=pltpu.CompilerParams(vmem_limit_bytes=4 << 20),
        cost_estimate=pl.CostEstimate(flops=550_000_000, bytes_accessed=1 << 20, transcendentals=0),
        name="clear",
    )()
    panel, cleared = lax.optimization_barrier((features.T, cleared))
    full = lax.all_gather(panel, "col", axis=0, tiled=True)
    z, scale = pl.pallas_call(
        transform_kernel,
        out_shape=(
            jax.ShapeDtypeStruct((outs, nodes), BF16),
            jax.ShapeDtypeStruct((8, nodes), F32),
        ),
        in_specs=[vmem] * 4,
        out_specs=(vmem,) * 2,
        compiler_params=pltpu.CompilerParams(vmem_limit_bytes=12 << 20),
        name="transform",
    )(block_count.reshape(1, -1), adjacency, full, weight.T)

    half = devices // 2

    def plus(s):
        return s + 1 if s + 1 < devices else None

    def minus(s):
        return s - 1 if s > 0 else None

    def pair(s):
        return (s + half) % devices

    def sum_blocks(mine, values, kept):
        shapes = (
            sums,
            sums,
            jax.ShapeDtypeStruct((outs, nodes), F32),
            jax.ShapeDtypeStruct((outs, 1), F32),
            jax.ShapeDtypeStruct((outs, nodes), BF16),
        )
        return pl.pallas_call(
            functools.partial(blocks_kernel, mine),
            out_shape=shapes,
            in_specs=[anywhere] * 3 + [vmem] * (2 + len(kept)),
            input_output_aliases={5 + i: i for i in range(len(kept))},
            out_specs=(vmem,) * 5,
            scratch_shapes=[
                pltpu.SMEM(block_count.shape, jnp.int32),
                pltpu.SMEM(block_cols.shape, jnp.int32),
                pltpu.VMEM(adjacency.shape, BF16),
                pltpu.SemaphoreType.DMA((3,)),
            ],
            compiler_params=pltpu.CompilerParams(vmem_limit_bytes=12 << 20),
            cost_estimate=pl.CostEstimate(flops=50_000_000, bytes_accessed=3 << 20, transcendentals=0),
            name="blocks",
        )(block_count, block_cols, adjacency, values, bias.reshape(1, -1), *kept)

    *kept, z = sum_blocks(lambda place: place < NEAR, z, cleared)

    def exchange(targets):
        return lax.ppermute(z, "row", [(s, targets(s)) for s in range(devices) if targets(s) is not None])

    before = exchange(plus)
    first = exchange(lambda s: pair(s) if s % LINE < NEAR or (s >= half and s % LINE < LINE - 1) else None)
    after = exchange(minus)
    last = exchange(lambda s: pair(s) if s % LINE == LINE - 1 or (s < half and s % LINE >= NEAR) else None)
    upper, lower, base, offset, _ = sum_blocks(lambda place: place >= NEAR, z, kept)
    out = pl.pallas_call(
        finish_kernel,
        out_shape=jax.ShapeDtypeStruct((outs, nodes), BF16),
        in_specs=[vmem] * 9,
        out_specs=vmem,
        compiler_params=pltpu.CompilerParams(vmem_limit_bytes=4 << 20),
        name="finish",
    )(last, after, first, before, upper, lower, base, scale, offset)
    return out.T


def solution(mesh):
    return jax.shard_map(
        on_device,
        mesh=mesh,
        in_specs=(
            P("row", "col"),
            P(None, "col"),
            P("col"),
            P("row", None, None, None),
            P("row", None),
            P("row"),
        ),
        out_specs=P("row", "col"),
        check_vma=False,
    )
```

```python
import functools

import jax
import jax.numpy as jnp
from jax import lax
from jax.experimental import pallas as pl
from jax.experimental.pallas import tpu as pltpu
from jax.sharding import PartitionSpec as P

F32 = jnp.float32
BF16 = jnp.bfloat16
VMEM = pltpu.MemorySpace.VMEM
NT = (((1,), (1,)), ((), ()))
LINE = 12
NEAR = 3
UNROLL = 3


def split(value):
    high = value.astype(BF16)
    return high, (value - high.astype(F32)).astype(BF16)


def clear_kernel(*out_refs):
    for ref in out_refs:
        ref[...] = jnp.zeros_like(ref)


def transform_kernel(count_ref, tiles, full_ref, weight_ref, z_ref, scale_ref):
    own_rows, kmax, bsize, _ = tiles.shape
    product = jnp.dot(weight_ref[...], full_ref[...], preferred_element_type=F32)
    sums = []
    for r in range(own_rows):
        count = jnp.broadcast_to(count_ref[:, r : r + 1], (8, bsize))
        total = jnp.zeros((bsize // 8, 8, bsize), F32)
        for k in range(kmax):
            live = jnp.where(count > k, 1.0, 0.0)
            total += tiles[r, k].astype(F32).reshape(total.shape) * live[None]
        sums.append(total.reshape(bsize, bsize))
    parts = jnp.concatenate(split(jnp.concatenate(sums, axis=0)), axis=1)
    ones = jnp.ones((16, 2 * bsize), BF16)
    degree = 1.0 + lax.dot_general(ones, parts, NT, preferred_element_type=F32)
    scale = lax.rsqrt(degree[:1, :])
    z_ref[...] = (product * scale).astype(BF16)
    scale_ref[...] = jnp.broadcast_to(scale, scale_ref.shape)


def square(blocks, slot):
    rows = [jnp.concatenate([ref[2 * slot], ref[2 * slot + 1]], axis=1) for ref in blocks]
    return jnp.concatenate(rows, axis=0)


def blocks_kernel(mine, count_any, cols_any, tiles_any, z_ref, bias_ref, *refs):
    upper_ref, lower_ref, base_ref, offset_ref, same_ref, count_ref, cols_ref, tiles, sems = refs[-9:]
    same_ref[...] = z_ref[...]

    @pl.when(mine(lax.rem(lax.axis_index("row"), LINE)))
    def _():
        loads = [
            pltpu.make_async_copy(count_any, count_ref, sems.at[0]),
            pltpu.make_async_copy(cols_any, cols_ref, sems.at[1]),
            pltpu.make_async_copy(tiles_any, tiles, sems.at[2]),
        ]
        for load in loads:
            load.start()
        for load in loads:
            load.wait()
        blocks = (upper_ref, lower_ref)
        own_rows = tiles.shape[0]
        first = lax.axis_index("row") * own_rows - 2
        spare = upper_ref.shape[0] - 1
        counts = [count_ref[r] for r in range(own_rows)]

        def add(r, k):
            place = jnp.where(k < counts[r], jnp.clip(cols_ref[r, k] - first, 0, 5), spare)
            blocks[r][place] += tiles[r, k]

        for r in range(own_rows):
            blocks[r][6 + r] = tiles[r, 1]
            add(r, 0)

        def step(k, _):
            for u in range(UNROLL):
                for r in range(own_rows):
                    add(r, 2 + k * UNROLL + u)
            return 0

        longest = jnp.maximum(counts[0], counts[1])
        lax.fori_loop(0, (longest - 2 + UNROLL - 1) // UNROLL, step, 0)
        own = z_ref[...]
        base_ref[...] = own.astype(F32) + lax.dot_general(own, square(blocks, 1), NT, preferred_element_type=F32)
        outs = bias_ref.shape[1]
        eye = lax.broadcasted_iota(jnp.int32, (outs, outs), 0) == lax.broadcasted_iota(jnp.int32, (outs, outs), 1)
        offset_ref[...] = jnp.sum(jnp.where(eye, bias_ref[...], 0.0), axis=1, keepdims=True)


def finish_kernel(
    last_ref, after_ref, first_ref, before_ref, upper_ref, lower_ref, base_ref, scale_ref, offset_ref, out_ref
):
    blocks = (upper_ref, lower_ref)
    total = base_ref[...]
    pair = first_ref[...] + last_ref[...]
    for slot, z in ((0, before_ref[...]), (2, after_ref[...]), (3, pair)):
        total += lax.dot_general(z, square(blocks, slot), NT, preferred_element_type=F32)
    result = scale_ref[:1, :] * total + offset_ref[...]
    out_ref[...] = jnp.maximum(result, 0.0).astype(BF16)


def on_device(features, weight, bias, adjacency, block_cols, block_count):
    own_rows, _, bsize, _ = adjacency.shape
    devices = lax.axis_size("row")
    nodes = features.shape[0]
    outs = weight.shape[1]
    vmem = pl.BlockSpec(memory_space=VMEM)
    anywhere = pl.BlockSpec(memory_space=pl.ANY)

    sums = jax.ShapeDtypeStruct((9, bsize, bsize), BF16)
    cleared = pl.pallas_call(
        clear_kernel,
        out_shape=(sums,) * own_rows,
        out_specs=(vmem,) * own_rows,
        compiler_params=pltpu.CompilerParams(vmem_limit_bytes=4 << 20),
        cost_estimate=pl.CostEstimate(flops=550_000_000, bytes_accessed=1 << 20, transcendentals=0),
        name="clear",
    )()
    panel, cleared = lax.optimization_barrier((features.T, cleared))
    full = lax.all_gather(panel, "col", axis=0, tiled=True)
    z, scale = pl.pallas_call(
        transform_kernel,
        out_shape=(
            jax.ShapeDtypeStruct((outs, nodes), BF16),
            jax.ShapeDtypeStruct((8, nodes), F32),
        ),
        in_specs=[vmem] * 4,
        out_specs=(vmem,) * 2,
        compiler_params=pltpu.CompilerParams(vmem_limit_bytes=12 << 20),
        name="transform",
    )(block_count.reshape(1, -1), adjacency, full, weight.T)

    half = devices // 2

    def plus(s):
        return s + 1 if s + 1 < devices else None

    def minus(s):
        return s - 1 if s > 0 else None

    def pair(s):
        return (s + half) % devices

    def sum_blocks(mine, values, kept):
        shapes = (
            sums,
            sums,
            jax.ShapeDtypeStruct((outs, nodes), F32),
            jax.ShapeDtypeStruct((outs, 1), F32),
            jax.ShapeDtypeStruct((outs, nodes), BF16),
        )
        return pl.pallas_call(
            functools.partial(blocks_kernel, mine),
            out_shape=shapes,
            in_specs=[anywhere] * 3 + [vmem] * (2 + len(kept)),
            input_output_aliases={5 + i: i for i in range(len(kept))},
            out_specs=(vmem,) * 5,
            scratch_shapes=[
                pltpu.SMEM(block_count.shape, jnp.int32),
                pltpu.SMEM(block_cols.shape, jnp.int32),
                pltpu.VMEM(adjacency.shape, BF16),
                pltpu.SemaphoreType.DMA((3,)),
            ],
            compiler_params=pltpu.CompilerParams(vmem_limit_bytes=12 << 20),
            cost_estimate=pl.CostEstimate(flops=50_000_000, bytes_accessed=3 << 20, transcendentals=0),
            name="blocks",
        )(block_count, block_cols, adjacency, values, bias.reshape(1, -1), *kept)

    *kept, z = sum_blocks(lambda place: place < NEAR, z, cleared)

    def exchange(targets):
        return lax.ppermute(z, "row", [(s, targets(s)) for s in range(devices) if targets(s) is not None])

    before = exchange(plus)
    first = exchange(lambda s: pair(s) if s % LINE < NEAR or (s >= half and s % LINE < LINE - 1) else None)
    after = exchange(minus)
    last = exchange(lambda s: pair(s) if s % LINE == LINE - 1 or (s < half and s % LINE >= NEAR) else None)
    upper, lower, base, offset, _ = sum_blocks(lambda place: place >= NEAR, z, kept)
    out = pl.pallas_call(
        finish_kernel,
        out_shape=jax.ShapeDtypeStruct((outs, nodes), BF16),
        in_specs=[vmem] * 9,
        out_specs=vmem,
        compiler_params=pltpu.CompilerParams(vmem_limit_bytes=4 << 20),
        name="finish",
    )(last, after, first, before, upper, lower, base, scale, offset)
    return out.T


def solution(mesh):
    return jax.shard_map(
        on_device,
        mesh=mesh,
        in_specs=(
            P("row", "col"),
            P(None, "col"),
            P("col"),
            P("row", None, None, None),
            P("row", None),
            P("row"),
        ),
        out_specs=P("row", "col"),
        check_vma=False,
    )
```

```python
import functools

import jax
import jax.numpy as jnp
from jax import lax
from jax.experimental import pallas as pl
from jax.experimental.pallas import tpu as pltpu
from jax.sharding import PartitionSpec as P

F32 = jnp.float32
BF16 = jnp.bfloat16
VMEM = pltpu.MemorySpace.VMEM
NT = (((1,), (1,)), ((), ()))
LINE = 12
NEAR = 9
UNROLL = 3


def split(value):
    high = value.astype(BF16)
    return high, (value - high.astype(F32)).astype(BF16)


def clear_kernel(*out_refs):
    for ref in out_refs:
        ref[...] = jnp.zeros_like(ref)


def transform_kernel(count_ref, tiles, full_ref, weight_ref, z_ref, scale_ref):
    own_rows, kmax, bsize, _ = tiles.shape
    product = jnp.dot(weight_ref[...], full_ref[...], preferred_element_type=F32)
    sums = []
    for r in range(own_rows):
        count = jnp.broadcast_to(count_ref[:, r : r + 1], (8, bsize))
        total = jnp.zeros((bsize // 8, 8, bsize), F32)
        for k in range(kmax):
            live = jnp.where(count > k, 1.0, 0.0)
            total += tiles[r, k].astype(F32).reshape(total.shape) * live[None]
        sums.append(total.reshape(bsize, bsize))
    parts = jnp.concatenate(split(jnp.concatenate(sums, axis=0)), axis=1)
    ones = jnp.ones((16, 2 * bsize), BF16)
    degree = 1.0 + lax.dot_general(ones, parts, NT, preferred_element_type=F32)
    scale = lax.rsqrt(degree[:1, :])
    z_ref[...] = (product * scale).astype(BF16)
    scale_ref[...] = jnp.broadcast_to(scale, scale_ref.shape)


def square(blocks, slot):
    rows = [jnp.concatenate([ref[2 * slot], ref[2 * slot + 1]], axis=1) for ref in blocks]
    return jnp.concatenate(rows, axis=0)


def blocks_kernel(mine, count_any, cols_any, tiles_any, z_ref, bias_ref, *refs):
    upper_ref, lower_ref, base_ref, offset_ref, same_ref, count_ref, cols_ref, tiles, sems = refs[-9:]
    same_ref[...] = z_ref[...]

    @pl.when(mine(lax.rem(lax.axis_index("row"), LINE)))
    def _():
        loads = [
            pltpu.make_async_copy(count_any, count_ref, sems.at[0]),
            pltpu.make_async_copy(cols_any, cols_ref, sems.at[1]),
            pltpu.make_async_copy(tiles_any, tiles, sems.at[2]),
        ]
        for load in loads:
            load.start()
        for load in loads:
            load.wait()
        blocks = (upper_ref, lower_ref)
        own_rows = tiles.shape[0]
        first = lax.axis_index("row") * own_rows - 2
        spare = upper_ref.shape[0] - 1
        counts = [count_ref[r] for r in range(own_rows)]

        def add(r, k):
            place = jnp.where(k < counts[r], jnp.clip(cols_ref[r, k] - first, 0, 5), spare)
            blocks[r][place] += tiles[r, k]

        for r in range(own_rows):
            blocks[r][6 + r] = tiles[r, 1]
            add(r, 0)

        def step(k, _):
            for u in range(UNROLL):
                for r in range(own_rows):
                    add(r, 2 + k * UNROLL + u)
            return 0

        longest = jnp.maximum(counts[0], counts[1])
        lax.fori_loop(0, (longest - 2 + UNROLL - 1) // UNROLL, step, 0)
        own = z_ref[...]
        base_ref[...] = own.astype(F32) + lax.dot_general(own, square(blocks, 1), NT, preferred_element_type=F32)
        outs = bias_ref.shape[1]
        eye = lax.broadcasted_iota(jnp.int32, (outs, outs), 0) == lax.broadcasted_iota(jnp.int32, (outs, outs), 1)
        offset_ref[...] = jnp.sum(jnp.where(eye, bias_ref[...], 0.0), axis=1, keepdims=True)


def finish_kernel(
    last_ref, after_ref, first_ref, before_ref, upper_ref, lower_ref, base_ref, scale_ref, offset_ref, out_ref
):
    blocks = (upper_ref, lower_ref)
    total = base_ref[...]
    pair = first_ref[...] + last_ref[...]
    for slot, z in ((0, before_ref[...]), (2, after_ref[...]), (3, pair)):
        total += lax.dot_general(z, square(blocks, slot), NT, preferred_element_type=F32)
    result = scale_ref[:1, :] * total + offset_ref[...]
    out_ref[...] = jnp.maximum(result, 0.0).astype(BF16)


def on_device(features, weight, bias, adjacency, block_cols, block_count):
    own_rows, _, bsize, _ = adjacency.shape
    devices = lax.axis_size("row")
    nodes = features.shape[0]
    outs = weight.shape[1]
    vmem = pl.BlockSpec(memory_space=VMEM)
    anywhere = pl.BlockSpec(memory_space=pl.ANY)

    sums = jax.ShapeDtypeStruct((9, bsize, bsize), BF16)
    cleared = pl.pallas_call(
        clear_kernel,
        out_shape=(sums,) * own_rows,
        out_specs=(vmem,) * own_rows,
        compiler_params=pltpu.CompilerParams(vmem_limit_bytes=4 << 20),
        cost_estimate=pl.CostEstimate(flops=550_000_000, bytes_accessed=1 << 20, transcendentals=0),
        name="clear",
    )()
    panel, cleared = lax.optimization_barrier((features.T, cleared))
    full = lax.all_gather(panel, "col", axis=0, tiled=True)
    z, scale = pl.pallas_call(
        transform_kernel,
        out_shape=(
            jax.ShapeDtypeStruct((outs, nodes), BF16),
            jax.ShapeDtypeStruct((8, nodes), F32),
        ),
        in_specs=[vmem] * 4,
        out_specs=(vmem,) * 2,
        compiler_params=pltpu.CompilerParams(vmem_limit_bytes=12 << 20),
        name="transform",
    )(block_count.reshape(1, -1), adjacency, full, weight.T)

    half = devices // 2

    def plus(s):
        return s + 1 if s + 1 < devices else None

    def minus(s):
        return s - 1 if s > 0 else None

    def pair(s):
        return (s + half) % devices

    def sum_blocks(mine, values, kept):
        shapes = (
            sums,
            sums,
            jax.ShapeDtypeStruct((outs, nodes), F32),
            jax.ShapeDtypeStruct((outs, 1), F32),
            jax.ShapeDtypeStruct((outs, nodes), BF16),
        )
        return pl.pallas_call(
            functools.partial(blocks_kernel, mine),
            out_shape=shapes,
            in_specs=[anywhere] * 3 + [vmem] * (2 + len(kept)),
            input_output_aliases={5 + i: i for i in range(len(kept))},
            out_specs=(vmem,) * 5,
            scratch_shapes=[
                pltpu.SMEM(block_count.shape, jnp.int32),
                pltpu.SMEM(block_cols.shape, jnp.int32),
                pltpu.VMEM(adjacency.shape, BF16),
                pltpu.SemaphoreType.DMA((3,)),
            ],
            compiler_params=pltpu.CompilerParams(vmem_limit_bytes=12 << 20),
            cost_estimate=pl.CostEstimate(flops=50_000_000, bytes_accessed=3 << 20, transcendentals=0),
            name="blocks",
        )(block_count, block_cols, adjacency, values, bias.reshape(1, -1), *kept)

    *kept, z = sum_blocks(lambda place: place < NEAR, z, cleared)

    def exchange(targets):
        return lax.ppermute(z, "row", [(s, targets(s)) for s in range(devices) if targets(s) is not None])

    before = exchange(plus)
    first = exchange(lambda s: pair(s) if s % LINE < NEAR or (s >= half and s % LINE < LINE - 1) else None)
    after = exchange(minus)
    last = exchange(lambda s: pair(s) if s % LINE == LINE - 1 or (s < half and s % LINE >= NEAR) else None)
    upper, lower, base, offset, _ = sum_blocks(lambda place: place >= NEAR, z, kept)
    out = pl.pallas_call(
        finish_kernel,
        out_shape=jax.ShapeDtypeStruct((outs, nodes), BF16),
        in_specs=[vmem] * 9,
        out_specs=vmem,
        compiler_params=pltpu.CompilerParams(vmem_limit_bytes=4 << 20),
        name="finish",
    )(last, after, first, before, upper, lower, base, scale, offset)
    return out.T


def solution(mesh):
    return jax.shard_map(
        on_device,
        mesh=mesh,
        in_specs=(
            P("row", "col"),
            P(None, "col"),
            P("col"),
            P("row", None, None, None),
            P("row", None),
            P("row"),
        ),
        out_specs=P("row", "col"),
        check_vma=False,
    )
```
